32 devices in a mesh: dp: 4 (over x, core), expert: 2 (over y), etp: 4 (over z).
Axes of the slice: x: 2, y: 2, z: 4, core: 2. Of those that a mesh axis runs over, the one named last changes fastest.
Arguments:
- tokens: bfloat16 [1024, 6144], P(('dp', 'expert'), 'etp'), may hold values from -6 to 6
- routes: int32 [1024, 2], P(('dp', 'expert')), may hold values from 0 to 1, as said below
- gate_scale: float32 [1024, 2], P(('dp', 'expert')), may hold values from 0.2 to 1
- gate_weight: bfloat16 [2, 128, 6, 128, 128], P('expert', 'etp'), may hold values from -0.21875 to 0.21875
- up_weight: bfloat16 [2, 128, 6, 128, 128], P('expert', 'etp'), may hold values from -0.21875 to 0.21875
- down_weight: bfloat16 [2, 16, 48, 128, 128], P('expert', 'etp'), may hold values from -0.125 to 0.125
- gate_blocks: int32 [2, 128, 6], P('expert', 'etp'), may hold values from 0 to 47, as said below
- down_blocks: int32 [2, 16, 48], P('expert', 'etp'), may hold values from 0 to 7
Outputs:
- mixed: bfloat16 [1024, 6144], P(('dp', 'expert'), 'etp')
The draws below stay inside these ranges and needn't reach their ends.
Inputs may be any that keep to these rules, and one draw needn't show every extreme that they name: `routes`: the two entries of a token name different experts. In each aligned block of 128 rows no expert is named more than 128 times, and one expert, the same for all blocks, is named exactly 128 times in every block. `gate_blocks`: for each expert and hidden block the 6 entries are different.
All inputs are finite; a program needn't handle non-finite values.
Results may differ from the reference program's by a relative error of at most 0.011.
Values may be sent and summed in bfloat16 or wider, within the bound.
No kernel may reach another device: no remote copies, remote signals or barrier semaphores. Data moves between devices by JAX's collectives and lax.ppermute only.
A program may use at most 128 MiB of HBM per device.

```python
import jax
import jax.numpy as jnp
from jax import lax

D = 6144
FF = 16384
BLK = 128
KEEP = 6
GROUP = 8
TOK_DEV = 128
EXPERTS = 2
TOKENS = 1024
CAP = 128
N_ETP = 4


def draw_routes(key, part):
    block_total = TOKENS // TOK_DEV
    favored = jax.random.randint(jax.random.fold_in(key, 1), (), 0, EXPERTS)
    expert_ids = jnp.arange(EXPERTS, dtype=jnp.int32)
    slack_total = EXPERTS * CAP - 2 * TOK_DEV

    def one_block(block_key):
        key_weight, key_order, key_rows, key_flip = jax.random.split(block_key, 4)
        others = expert_ids != favored
        weights = jnp.where(others, jax.random.randint(key_weight, (EXPERTS,), 1, 5), 0)
        deficit = slack_total * weights // jnp.sum(weights)
        remains = slack_total - jnp.sum(deficit)
        rank_other = jnp.cumsum(others.astype(jnp.int32)) - 1
        deficit = deficit + jnp.where(others & (rank_other < remains), 1, 0)
        counts = CAP - deficit
        ordering = jax.random.permutation(key_order, EXPERTS)
        bounds = jnp.cumsum(counts[ordering])
        position = jnp.arange(2 * TOK_DEV)
        which_slot = jnp.sum((position[:, None] >= bounds[None, :]).astype(jnp.int32), axis=1)
        labels = ordering[which_slot].reshape(2, TOK_DEV).T
        labels = labels[jax.random.permutation(key_rows, TOK_DEV)]
        flipped = jax.random.randint(key_flip, (TOK_DEV, 1), 0, 2)
        labels = jnp.where(flipped == 1, labels[:, ::-1], labels)
        return labels
    block_keys = jax.random.split(jax.random.fold_in(key, 2), block_total)
    return jax.vmap(one_block)(block_keys).reshape(TOKENS, 2).astype(jnp.int32)


def draw_gate_blocks(key, part):
    block_keys = jax.random.split(jax.random.fold_in(key, 11), EXPERTS * (FF // BLK))

    def pick_blocks(block_key):
        return jax.random.permutation(block_key, D // BLK)[:KEEP]
    picks = jax.vmap(pick_blocks)(block_keys)
    return picks.reshape(EXPERTS, FF // BLK, KEEP).astype(jnp.int32)


def touch_ends(result, key, least, top_value):
    dims = result.shape
    index_at = [jax.random.randint(jax.random.fold_in(key, axis), (), 0, dims[axis]) for axis in range(len(dims))]
    result = result.at[tuple(index_at)].set(least)
    longest = dims.index(max(dims))
    index_at[longest] = (index_at[longest] + 1) % dims[longest]
    return result.at[tuple(index_at)].set(top_value)


def block_scale(own_key, extent, shards, low, top_value):
    loudness = 1.0
    for axis_at, shards_of in shards:
        heights = jax.random.uniform(jax.random.fold_in(jax.random.fold_in(own_key, 6), axis_at), (shards_of,), jnp.float32, low / len(shards), top_value / len(shards))
        loudness = loudness * jnp.repeat(jnp.exp(heights), extent[axis_at] // shards_of).reshape((-1,) + (1,) * (len(extent) - 1 - axis_at))
    return loudness


def bell_draw(stream_key, extent, spread, bound, shards=(), kind=jnp.bfloat16):
    factor_of = block_scale(stream_key, extent, shards, -0.22, 0.18) if shards else 1.0
    result = jax.random.normal(stream_key, extent, jnp.float32) * spread * factor_of
    return jnp.minimum(jnp.maximum(result, -bound), bound).astype(kind)


def setup_inputs(seed: int = 0) -> dict:
    key_of = jax.random.split(jax.random.key(seed), 9)
    tokens = bell_draw(key_of[0], (TOKENS, D), 1.0, 6.0, ((0, 8), (1, 4)))
    routes = draw_routes(jax.random.fold_in(key_of[8], 71), 0)
    gate_scale = jnp.clip(0.2 + 0.8 * jax.random.uniform(key_of[2], (TOKENS, 2), jnp.float32) ** block_scale(key_of[2], (TOKENS, 2), ((0, 8),), -0.2, 0.2), 0.2, 1.0)
    gate_weight = bell_draw(key_of[3], (EXPERTS, FF // BLK, KEEP, BLK, BLK), (KEEP * BLK) ** -0.5, 0.21875, ((0, 2), (1, 4)))
    up_weight = bell_draw(key_of[4], (EXPERTS, FF // BLK, KEEP, BLK, BLK), (KEEP * BLK) ** -0.5, 0.21875, ((0, 2), (1, 4)))
    down_weight = bell_draw(key_of[5], (EXPERTS, FF // (GROUP * BLK), D // BLK, BLK, BLK), (FF // GROUP) ** -0.5, 0.125, ((0, 2), (1, 4)))
    gate_blocks = draw_gate_blocks(jax.random.fold_in(key_of[8], 71), 0)
    down_blocks = touch_ends(jax.random.randint(key_of[7], (EXPERTS, FF // (GROUP * BLK), D // BLK), 0, GROUP), jax.random.fold_in(key_of[7], 1), 0, GROUP - 1).astype(jnp.int32)
    return dict(tokens=tokens, routes=routes, gate_scale=gate_scale, gate_weight=gate_weight, up_weight=up_weight, down_weight=down_weight, gate_blocks=gate_blocks, down_blocks=down_blocks)


def slot_places(route_rows, expert_count, capacity):
    flat_routes = route_rows.reshape(-1)
    onehot = (flat_routes[:, None] == jnp.arange(expert_count, dtype=jnp.int32)[None, :]).astype(jnp.int32)
    earlier = (jnp.cumsum(onehot, axis=0) - onehot).astype(jnp.int32)
    slot_place = jnp.sum(earlier * onehot, axis=1).astype(jnp.int32)
    return (flat_routes * capacity + slot_place).astype(jnp.int32)


def expert_share(token_rows, gate_part, up_part, down_part, gate_pick, down_pick):
    row_count = token_rows.shape[0]
    hidden_count = gate_part.shape[0]
    group_count = down_part.shape[0]
    tiles = token_rows.reshape(row_count, D // BLK, BLK)
    picked = jnp.take(tiles, gate_pick.reshape(-1), axis=1).reshape(row_count, hidden_count, KEEP, BLK)
    picked = picked.astype(jnp.float32)
    gate_act = jnp.einsum("rfki,fkio->rfo", picked, gate_part.astype(jnp.float32))
    up_act = jnp.einsum("rfki,fkio->rfo", picked, up_part.astype(jnp.float32))
    hidden = (jax.nn.silu(gate_act) * up_act).astype(jnp.bfloat16)
    sources = down_pick + (jnp.arange(group_count, dtype=jnp.int32) * GROUP)[:, None]
    chosen = jnp.take(hidden, sources.reshape(-1), axis=1).reshape(row_count, group_count, D // BLK, BLK)
    partial_value = jnp.einsum("rgbi,gbio->rbo", chosen.astype(jnp.float32), down_part.astype(jnp.float32))
    return partial_value.reshape(row_count, D)


def one_expert(token_rows, gate_part, up_part, down_part, gate_pick, down_pick):
    per_slice = FF // BLK // N_ETP
    group_slice = FF // (GROUP * BLK) // N_ETP

    def add_slice(slice_index, total):
        hidden_start = (slice_index * per_slice).astype(jnp.int32)
        group_start = (slice_index * group_slice).astype(jnp.int32)
        share = expert_share(
            token_rows,
            lax.dynamic_slice_in_dim(gate_part, hidden_start, per_slice, 0),
            lax.dynamic_slice_in_dim(up_part, hidden_start, per_slice, 0),
            lax.dynamic_slice_in_dim(down_part, group_start, group_slice, 0),
            lax.dynamic_slice_in_dim(gate_pick, hidden_start, per_slice, 0),
            lax.dynamic_slice_in_dim(down_pick, group_start, group_slice, 0),
        )
        rounded = lax.optimization_barrier(share.astype(jnp.bfloat16))
        return total + rounded.astype(jnp.float32)

    total = lax.fori_loop(0, N_ETP, add_slice, jnp.zeros((token_rows.shape[0], D), jnp.float32))
    return total.astype(jnp.bfloat16)


def run_expert(operands):
    return one_expert(*operands)


def anchor_of(dest_row):
    filler = jnp.full((EXPERTS * CAP,), TOK_DEV, jnp.int32)
    return filler.at[dest_row].set(jnp.arange(2 * TOK_DEV, dtype=jnp.int32) // 2)


def take_rows(block_rows, indices):
    return jnp.take(block_rows, indices, axis=0, mode="fill", fill_value=0)


def fetch_rows(block_rows, indices):
    return jnp.take(block_rows, indices, axis=0)


def block_places(route_rows):
    return slot_places(route_rows, EXPERTS, CAP)


def reference(tokens, routes, gate_scale, gate_weight, up_weight, down_weight, gate_blocks, down_blocks):
    blocks_all = TOKENS // TOK_DEV
    tok_blocks = tokens.reshape(blocks_all, TOK_DEV, D)
    route_blocks = routes.reshape(blocks_all, TOK_DEV, 2)
    destination = jax.vmap(block_places)(route_blocks)
    anchor = jax.vmap(anchor_of)(destination)
    gathered = jax.vmap(take_rows)(tok_blocks, anchor)
    by_expert = gathered.reshape(blocks_all, EXPERTS, CAP, D).transpose(1, 0, 2, 3).reshape(EXPERTS, blocks_all * CAP, D)
    outputs = lax.map(run_expert, (by_expert, gate_weight, up_weight, down_weight, gate_blocks, down_blocks))
    returned = outputs.reshape(EXPERTS, blocks_all, CAP, D).transpose(1, 0, 2, 3).reshape(blocks_all, EXPERTS * CAP, D)
    fetched = jax.vmap(fetch_rows)(returned, destination)
    fetched = fetched.reshape(TOKENS, 2, D).astype(jnp.float32)
    mixed = jnp.sum(fetched * gate_scale[:, :, None], axis=1)
    return mixed.astype(jnp.bfloat16)
```

```python
import functools

import jax
import jax.numpy as jnp
from jax import lax
from jax.experimental import pallas as pl
from jax.experimental.pallas import tpu as pltpu
from jax.sharding import PartitionSpec as P


def slot_places(route_rows, expert_count, capacity):
    flat_routes = route_rows.reshape(-1)
    onehot = (flat_routes[:, None] == jnp.arange(expert_count, dtype=jnp.int32)[None, :]).astype(
        jnp.int32
    )
    earlier = jnp.cumsum(onehot, axis=0) - onehot
    slot_place = jnp.sum(earlier * onehot, axis=1)
    return flat_routes * capacity + slot_place


def expert_layer(token_rows, gate_part, up_part, down_part, gate_pick, down_pick):
    row_count = token_rows.shape[0]
    model_width = token_rows.shape[1]
    block_size = gate_part.shape[-1]
    hidden_count = gate_part.shape[0]
    keep_count = gate_part.shape[1]
    group_count = down_part.shape[0]
    group_size = hidden_count // group_count
    tiles = token_rows.reshape(row_count, model_width // block_size, block_size)
    picked = jnp.take(tiles, gate_pick.reshape(-1), axis=1).reshape(
        row_count, hidden_count, keep_count, block_size
    )
    gate_act = jnp.einsum("rfki,fkio->rfo", picked, gate_part, preferred_element_type=jnp.float32)
    up_act = jnp.einsum("rfki,fkio->rfo", picked, up_part, preferred_element_type=jnp.float32)
    hidden = (jax.nn.silu(gate_act) * up_act).astype(jnp.bfloat16)
    sources = down_pick + (jnp.arange(group_count, dtype=jnp.int32) * group_size)[:, None]
    chosen = jnp.take(hidden, sources.reshape(-1), axis=1).reshape(
        row_count, group_count, model_width // block_size, block_size
    )
    partial_value = jnp.einsum(
        "rgbi,gbio->rbo", chosen, down_part, preferred_element_type=jnp.float32
    )
    return partial_value.reshape(row_count, model_width)


def general_body(
    tokens, routes, gate_scale, gate_weight, up_weight, down_weight, gate_blocks, down_blocks
):
    tok_count = tokens.shape[0]
    local_width = tokens.shape[1]
    group_total = lax.axis_size("expert")
    capacity = min(tok_count, 5 * tok_count // (2 * group_total))
    destination = slot_places(routes, group_total, capacity)
    filler = jnp.full((group_total * capacity,), tok_count, jnp.int32)
    anchor = filler.at[destination].set(jnp.arange(2 * tok_count, dtype=jnp.int32) // 2)
    outgoing = jnp.take(tokens, anchor, axis=0, mode="fill", fill_value=0)
    outgoing = outgoing.reshape(group_total, capacity, local_width)
    incoming = lax.all_to_all(outgoing, "expert", split_axis=0, concat_axis=0, tiled=True)
    arrived = lax.all_gather(incoming, "etp", axis=2, tiled=True)
    full_width = arrived.shape[2]
    partial_value = expert_layer(
        arrived.reshape(group_total * capacity, full_width),
        gate_weight[0],
        up_weight[0],
        down_weight[0],
        gate_blocks[0],
        down_blocks[0],
    )
    partial_value = partial_value.reshape(group_total, capacity, full_width)
    summed = lax.psum_scatter(
        partial_value.astype(jnp.bfloat16), "etp", scatter_dimension=2, tiled=True
    )
    returned = lax.all_to_all(summed, "expert", split_axis=0, concat_axis=0, tiled=True)
    returned = returned.reshape(group_total * capacity, local_width)
    fetched = (
        jnp.take(returned, destination, axis=0)
        .reshape(tok_count, 2, local_width)
        .astype(jnp.float32)
    )
    mixed = jnp.sum(fetched * gate_scale[:, :, None], axis=1)
    return mixed.astype(jnp.bfloat16)


def expert_kernel(
    n_slots, steps, per_step, keep, groups, group_size,
    pick_ref, down_ref, order_ref,
    *refs,
):
    pieces = refs[:n_slots]
    gate_ref, up_ref, weight_ref = refs[n_slots:n_slots + 3]
    out_ref = refs[n_slots + 3]
    rows_ref, hidden_ref, sems = refs[n_slots + 4:]
    step = pl.program_id(0)
    width = pieces[0].shape[1]
    blk = gate_ref.shape[-1]

    @pl.when(step == 0)
    def _():
        copies = [
            pltpu.make_async_copy(pieces[k], rows_ref.at[:, pl.ds(k * width, width)], sems.at[k])
            for k in range(n_slots)
        ]
        for c in copies:
            c.start()
        for c in copies:
            c.wait()

    @pl.when(step < steps)
    def _():
        for i in range(per_step):
            f = step * per_step + i
            xs = []
            for k in range(keep):
                at = pl.multiple_of(pick_ref[f * keep + k] * blk, blk)
                xs.append(rows_ref[:, pl.ds(at, blk)])
            x = jnp.concatenate(xs, axis=1)
            w = jnp.concatenate(
                [gate_ref[i].reshape(keep * blk, blk), up_ref[i].reshape(keep * blk, blk)], axis=1
            )
            both = jnp.dot(x, w, preferred_element_type=jnp.float32)
            g = both[:, :blk]
            u = both[:, blk:]
            h = g / (1.0 + jnp.exp(-g)) * u
            hidden_ref[f] = h.astype(jnp.bfloat16)

    @pl.when(step >= steps)
    def _():
        blocks = width // blk
        base = order_ref[step - steps] * blocks
        total = n_slots * blocks
        for b in range(blocks):
            hs = []
            for g in range(groups):
                at = down_ref[g * total + base + b] + g * group_size
                hs.append(hidden_ref[at])
            h = jnp.concatenate(hs, axis=1)
            w = weight_ref[:, b].reshape(groups * blk, blk)
            out_ref[0, :, b * blk:(b + 1) * blk] = jnp.dot(
                h, w, preferred_element_type=jnp.float32
            ).astype(jnp.bfloat16)


def run_expert(pieces, gate_part, up_part, down_part, picks, down_pick, order):
    n_slots = len(pieces)
    rows, width = pieces[0].shape
    hidden_count, keep, blk = gate_part.shape[:3]
    groups = down_part.shape[0]
    blocks = width // blk
    per_step = 4
    while hidden_count % per_step:
        per_step //= 2
    steps = hidden_count // per_step
    kernel = functools.partial(
        expert_kernel, n_slots, steps, per_step, keep, groups, hidden_count // groups
    )
    up_map = lambda i, p, d, o: (jnp.minimum(i, steps - 1), 0, 0, 0)
    down_map = lambda i, p, d, o: (0, o[jnp.maximum(i - steps, 0)], 0, 0)
    return pl.pallas_call(
        kernel,
        out_shape=jax.ShapeDtypeStruct((n_slots, rows, width), jnp.bfloat16),
        grid_spec=pltpu.PrefetchScalarGridSpec(
            num_scalar_prefetch=3,
            grid=(steps + n_slots,),
            in_specs=[pl.BlockSpec(memory_space=pl.ANY)] * n_slots
            + [
                pl.BlockSpec((per_step, keep, blk, blk), up_map),
                pl.BlockSpec((per_step, keep, blk, blk), up_map),
                pl.BlockSpec((groups, blocks, blk, blk), down_map),
            ],
            out_specs=pl.BlockSpec(
                (1, rows, width), lambda i, p, d, o: (jnp.maximum(i - steps, 0), 0, 0)
            ),
            scratch_shapes=[
                pltpu.VMEM((rows, n_slots * width), jnp.bfloat16),
                pltpu.VMEM((hidden_count, rows, blk), jnp.bfloat16),
                pltpu.SemaphoreType.DMA((n_slots,)),
            ],
        ),
        compiler_params=pltpu.CompilerParams(vmem_limit_bytes=32 * 1024 * 1024),
        name="expert",
    )(picks, down_pick, order, *pieces, gate_part, up_part, down_part)


def paired_body(
    tokens, routes, gate_scale, gate_weight, up_weight, down_weight, gate_blocks, down_blocks
):
    n = lax.axis_size("etp")
    z = lax.axis_index("etp")
    mine = lax.axis_index("expert")
    blocks = tokens.shape[1] // gate_weight.shape[-1]
    over_etp = lambda v, k: lax.ppermute(v, "etp", [(i, i ^ k) for i in range(n)])
    over_expert = lambda v: lax.ppermute(v, "expert", [(0, 1), (1, 0)])

    own = [tokens] + [over_etp(tokens, k) for k in range(1, n)]
    mate = [over_expert(v) for v in own]

    pick = gate_blocks[0]
    picks = (((pick // blocks) ^ z) * blocks + pick % blocks).reshape(-1)
    down_pick = down_blocks[0].reshape(-1)
    order = jnp.arange(n, dtype=jnp.int32) ^ z
    weights = (gate_weight[0], up_weight[0], down_weight[0], picks, down_pick, order)
    kept = run_expert(own, *weights)
    sent = run_expert(mate, *weights)

    factor = lambda e: jnp.sum(jnp.where(routes == e, gate_scale, 0.0), axis=1)[:, None]
    scale_mine = factor(mine)
    scale_other = factor(1 - mine)

    def joined(k):
        back = over_expert(sent[k])
        return scale_mine * kept[k].astype(jnp.float32) + scale_other * back.astype(jnp.float32)

    parts = [over_etp(joined(k).astype(jnp.bfloat16), k) for k in reversed(range(1, n))]
    mixed = joined(0)
    for part in parts:
        mixed = mixed + part.astype(jnp.float32)
    return mixed.astype(jnp.bfloat16)


def solution(mesh):
    n = mesh.shape["etp"]
    paired = mesh.shape["expert"] == 2 and n & (n - 1) == 0
    placed = (
        P(("dp", "expert"), "etp"),
        P(("dp", "expert"), None),
        P(("dp", "expert"), None),
        P("expert", "etp", None, None, None),
        P("expert", "etp", None, None, None),
        P("expert", "etp", None, None, None),
        P("expert", "etp", None),
        P("expert", "etp", None),
    )
    return jax.shard_map(
        paired_body if paired else general_body,
        mesh=mesh,
        in_specs=placed,
        out_specs=P(("dp", "expert"), "etp"),
        check_vma=False,
    )
```
